32 devices in a mesh: dp: 4 (over z), expert: 8 (over y, x, core).
Axes of the slice: x: 2, y: 2, z: 4, core: 2. Of those that a mesh axis runs over, the one named last changes fastest.
Arguments:
- tokens: bfloat16 [4096, 2048], P(('dp', 'expert')), may hold values from -6 to 6
- expert_ids: int32 [4096, 1], P(('dp', 'expert')), may hold values from 0 to 7; in each aligned block of 128 rows (0 to 127, 128 to 255, ...) at most 32 rows name the same one
- route_weights: bfloat16 [4096, 1], P(('dp', 'expert')), may hold values from 0.099609375 to 1
- out_grad: bfloat16 [4096, 2048], P(('dp', 'expert')), may hold values from -6 to 6
- gate_weight: bfloat16 [8, 768, 2048], P('expert'), may hold values from -0.125 to 0.125
- down_weight: bfloat16 [8, 768, 2048], P('expert'), may hold values from -0.21875 to 0.21875
Outputs:
- token_grad: bfloat16 [4096, 2048], P(('dp', 'expert'))
- route_grad: bfloat16 [4096, 1], P(('dp', 'expert'))
- gate_grad: bfloat16 [8, 768, 2048], P('expert', 'dp')
- down_grad: bfloat16 [8, 768, 2048], P('expert', 'dp')
The draws below stay inside these ranges and needn't reach their ends.
Inputs may be any that keep to these rules, and one draw needn't show every extreme that they name: `expert_ids`: the 1 expert of a token differ. Among the 128 tokens of one device no expert is named more than 32 times, a bound that some block reaches.
All inputs are finite; a program needn't handle non-finite values.
Results may differ from the reference program's by a relative error of at most 0.015.
Values may be sent and summed in bfloat16 or wider, within the bound.
A program may use at most 64 MiB of HBM per device.

```python
import math
import jax
import jax.numpy as jnp
import numpy as np
from jax import lax

D = 2048
FF = 768
TOP = 1
TOK_DEV = 128
EXPERTS = 8
CAPACITY = 32
TOKENS = 4096
N_DP = 4
N_EXPERT = 8


def levels(key, extent, pieces, smallest, high):
    loudness, own = 1.0, jax.random.fold_in(key, 6)
    for dim, parts in pieces:
        steps = jnp.exp(jax.random.uniform(jax.random.fold_in(own, dim), (parts,), jnp.float32, smallest / len(pieces), high / len(pieces)))
        loudness = loudness * jnp.repeat(steps, extent[dim] // parts).reshape([-1 if axis == dim else 1 for axis in range(len(extent))])
    return loudness


def deal_out(own_key, own, number, rows, number_of, top, limit, lean):
    sequence = jax.random.permutation(own_key, number_of)
    packed, common = portions_of(number_of, rows * top, limit, lean, True), portions_of(number_of, rows * top, limit, lean, False)
    places = jnp.arange(number_of)

    def named(tallies, turn):
        used = int((tallies > 0).sum())
        fixed = max(1, used // 4)
        passed = fixed + (places - fixed + turn * (used - fixed)) % max(1, number_of - fixed)
        return jnp.zeros((number_of,), jnp.int32).at[sequence[jnp.where(places < fixed, places, passed)]].set(jnp.asarray(tallies, jnp.int32))

    tallies = jnp.where(number % 4 == 0, named(packed, number // 4), named(common, number - number // 4 - 1))
    mixed = jax.random.permutation(jax.random.fold_in(own, 3), number_of)
    source_of, taker = mixed[0:number_of // 2 * 2:2], mixed[1:number_of // 2 * 2:2]
    slack = jnp.minimum(tallies[source_of] - 1, limit - tallies[taker]) // 2
    slack = jnp.where((source_of == sequence[0]) | (taker == sequence[0]) | (tallies[taker] == 0), 0, jnp.maximum(slack, 0))
    passed = jax.random.randint(jax.random.fold_in(own, 4), (number_of // 2,), 0, 1 << 20) % (slack + 1)
    tallies = tallies.at[source_of].add(-passed).at[taker].add(passed)
    members = jnp.searchsorted(jnp.cumsum(tallies), jnp.arange(rows * top), side="right").astype(jnp.int32)
    listing = members.reshape(top, rows).T
    listing = listing[jax.random.permutation(jax.random.fold_in(own, 1), rows)]
    turn = jax.random.randint(jax.random.fold_in(own, 2), (rows, 1), 0, top)
    return jnp.take_along_axis(listing, (jnp.arange(top)[None, :] + turn) % top, axis=1)


def portions_of(count, total, reach, skew, full):
    portions = [(1 << 20) // math.isqrt(grade ** skew) + 1 for grade in range(1, count + 1)]
    largest = reach if full else min(reach, max(-(-total // count), total * portions[0] // sum(portions)))
    least = 1 if total - largest >= count - 1 else 0
    counts, spare = [largest] + [least] * (count - 1), total - largest - least * (count - 1)
    while spare > 0:
        candidates = [i for i in range(1, count) if counts[i] < largest] or [i for i in range(1, count) if counts[i] < reach]
        pool, budget = sum([portions[i] for i in candidates]), spare
        for i in candidates:
            extra = min(reach - counts[i], max(1, budget * portions[i] // pool), spare)
            counts[i] = counts[i] + extra
            spare = spare - extra
    return np.array(counts)


def scatter_about(rng, dims, width, limit, split=(), kind=jnp.bfloat16):
    result = jax.random.normal(rng, dims, jnp.float32) * width
    if len(split) > 0:
        result = levels(rng, dims, split, -0.22, 0.18) * result
    return jnp.clip(result, min=-limit, max=limit).astype(kind)


def setup_inputs(seed: int = 0) -> dict:
    key_of = jax.random.split(jax.random.key(seed), 7)
    tokens = scatter_about(key_of[0], (TOKENS, D), 1.0, 6.0, ((0, 32),))
    expert_ids_keys = jax.random.split(jax.random.fold_in(key_of[1], 1), TOKENS // TOK_DEV)
    expert_ids_turns = jax.random.permutation(jax.random.fold_in(key_of[1], 3), TOKENS // TOK_DEV)
    expert_ids = jax.vmap(lambda own, number: deal_out(jax.random.fold_in(key_of[1], 2), own, number, TOK_DEV, EXPERTS, TOP, CAPACITY, 2))(expert_ids_keys, expert_ids_turns).reshape((TOKENS, TOP))
    route_weights = jnp.clip(0.099609375 + 0.9003906 * jax.random.uniform(key_of[2], (TOKENS, TOP), jnp.float32) ** levels(key_of[2], (TOKENS, TOP), ((0, 32),), -0.2, 0.2), 0.099609375, 1.0).astype(jnp.bfloat16)
    out_grad = scatter_about(key_of[3], (TOKENS, D), 1.0, 6.0, ((0, 32),))
    gate_weight = scatter_about(key_of[4], (EXPERTS, FF, D), D ** -0.5, 0.125, ((0, 8),))
    down_weight = scatter_about(key_of[5], (EXPERTS, FF, D), FF ** -0.5, 0.21875, ((0, 8),))
    return {"tokens": tokens, "expert_ids": expert_ids, "route_weights": route_weights, "out_grad": out_grad, "gate_weight": gate_weight, "down_weight": down_weight}


def silu_slope(values):
    sigma = jax.nn.sigmoid(values)
    return sigma * (1.0 + values * (1.0 - sigma))


def reference(tokens, expert_ids, route_weights, out_grad, gate_weight, down_weight):
    devices = TOKENS // TOK_DEV
    per_device = TOK_DEV * TOP
    work_rows = N_EXPERT * CAPACITY
    routed = expert_ids.reshape(devices, per_device)
    one_hot = (routed[:, :, None] == jnp.arange(EXPERTS, dtype=jnp.int32)[None, None, :]).astype(jnp.int32)
    ranking = jnp.sum((jnp.cumsum(one_hot, axis=1) - 1) * one_hot, axis=2)
    device_index = jnp.arange(devices, dtype=jnp.int32)[:, None]
    replica = device_index // N_EXPERT
    source = device_index % N_EXPERT
    position = ((routed * N_DP + replica) * N_EXPERT + source) * CAPACITY + ranking
    pair_index = device_index * per_device + jnp.arange(per_device, dtype=jnp.int32)[None, :]
    total_slots = EXPERTS * N_DP * work_rows
    slot_pair = jnp.full((total_slots,), -1, jnp.int32).at[position.reshape(-1)].set(pair_index.reshape(-1))
    slot_pair = slot_pair.reshape(EXPERTS, N_DP, work_rows)
    weights_flat = route_weights.reshape(-1)

    def expert_work(operands):
        pairs, gate, down = operands

        def replica_work(running, pair_rows):
            valid = pair_rows >= 0
            safe = jnp.maximum(pair_rows, 0)
            token_rows = safe // TOP
            inputs = jnp.where(valid[:, None], tokens[token_rows], jnp.zeros((), jnp.bfloat16))
            upstream = jnp.where(valid[:, None], out_grad[token_rows], jnp.zeros((), jnp.bfloat16))
            scales = jnp.where(valid, weights_flat[safe], jnp.zeros((), jnp.bfloat16))
            preact = jnp.dot(inputs, gate.T, preferred_element_type=jnp.float32)
            hidden = jax.nn.silu(preact).astype(jnp.bfloat16)
            outputs = jnp.dot(hidden, down, preferred_element_type=jnp.float32)
            prob_rows = jnp.sum(upstream.astype(jnp.float32) * outputs, axis=1).astype(jnp.bfloat16)
            scaled = (scales.astype(jnp.float32)[:, None] * upstream.astype(jnp.float32)).astype(jnp.bfloat16)
            hidden_grad = jnp.dot(scaled, down.T, preferred_element_type=jnp.float32)
            pre_grad = (hidden_grad * silu_slope(preact)).astype(jnp.bfloat16)
            input_grad = jnp.dot(pre_grad, gate, preferred_element_type=jnp.float32).astype(jnp.bfloat16)
            gate_term = jnp.dot(pre_grad.T, inputs, preferred_element_type=jnp.float32).astype(jnp.bfloat16)
            down_term = jnp.dot(hidden.T, scaled, preferred_element_type=jnp.float32).astype(jnp.bfloat16)
            gate_term, down_term = lax.optimization_barrier((gate_term, down_term))
            running_gate, running_down = running
            updated = (running_gate + gate_term.astype(jnp.float32), running_down + down_term.astype(jnp.float32))
            return updated, (input_grad, prob_rows)

        start = (jnp.zeros((FF, D), jnp.float32), jnp.zeros((FF, D), jnp.float32))
        summed, (input_grads, prob_rows) = lax.scan(replica_work, start, pairs)
        return summed[0].astype(jnp.bfloat16), summed[1].astype(jnp.bfloat16), input_grads, prob_rows

    gate_grad, down_grad, input_grads, prob_rows = lax.map(expert_work, (slot_pair, gate_weight, down_weight))
    flat_position = position.reshape(-1)
    pair_grads = input_grads.reshape(-1, D)[flat_position].astype(jnp.float32)
    token_grad = jnp.sum(pair_grads.reshape(TOKENS, TOP, D), axis=1).astype(jnp.bfloat16)
    route_grad = prob_rows.reshape(-1)[flat_position].reshape(TOKENS, TOP)
    return token_grad, route_grad, gate_grad, down_grad
```

```python
import functools

import jax
import jax.numpy as jnp
from jax import lax
from jax.experimental import pallas as pl
from jax.experimental.pallas import tpu as pltpu
from jax.sharding import PartitionSpec as P

MESH = pl.DeviceIdType.MESH
BF16, F32 = jnp.bfloat16, jnp.float32
LANES = 128


def kernel(
    n_dp, n_exp, cap, pieces,
    ids_ref, tokens_ref, weights_ref, grads_ref, gate_hbm, down_hbm,
    token_out, route_out, gate_out, down_out,
    sent, got, gate, down, preact, hid_t, da_t, back, returned, right_buf, left_buf,
    load_sem, send_sem, recv_sem, back_send, back_recv, r_send, r_recv, l_send, l_recv,
):
    rows, width = tokens_ref.shape
    slots = n_exp * cap
    units = gate.shape[0]
    part = units // n_dp
    piece = width // pieces
    tile = 256 if units % 256 == 0 else part
    r = lax.axis_index("dp")
    me = lax.axis_index("expert")

    def peer(k):
        return lax.rem(me + k, n_exp)

    def block(e):
        return pl.ds(pl.multiple_of(e * cap, cap), cap)

    loads = [
        pltpu.make_async_copy(gate_hbm, gate, load_sem.at[0]),
        pltpu.make_async_copy(down_hbm, down, load_sem.at[1]),
    ]
    for load in loads:
        load.start()

    barrier = pltpu.get_barrier_semaphore()

    @pl.loop(1, n_exp)
    def _(k):
        pl.semaphore_signal(barrier, inc=1, device_id={"expert": peer(k)}, device_id_type=MESH)

    up, low = lax.rem(r + 1, n_dp), lax.rem(r + n_dp - 1, n_dp)
    for other in (up, low):
        pl.semaphore_signal(barrier, inc=1, device_id={"dp": other}, device_id_type=MESH)

    ids = ids_ref[...]
    names = lax.broadcasted_iota(jnp.int32, (max(n_exp, 16), rows), 0)
    one_hot = (names == ids).astype(F32)
    before = (
        lax.broadcasted_iota(jnp.int32, (rows, rows), 0)
        < lax.broadcasted_iota(jnp.int32, (rows, rows), 1)
    ).astype(F32)
    counts = jnp.dot(one_hot.astype(BF16), before.astype(BF16), preferred_element_type=F32)
    rank = jnp.sum(counts * one_hot, axis=0, keepdims=True).astype(jnp.int32)
    target = ids * cap + rank
    place = (lax.broadcasted_iota(jnp.int32, (slots, rows), 0) == target).astype(F32).astype(BF16)

    sent[0] = jnp.dot(place, tokens_ref[...], preferred_element_type=F32).astype(BF16)
    pl.semaphore_wait(barrier, n_exp - 1 + 2)

    def exchange(t, k):
        to = peer(k)
        return pltpu.make_async_remote_copy(
            src_ref=sent.at[t, block(to)],
            dst_ref=got.at[t, block(me)],
            send_sem=send_sem.at[t, to],
            recv_sem=recv_sem.at[t, me],
            device_id={"expert": to},
            device_id_type=MESH,
        )

    def arrival(t, k):
        of = peer(k)
        return pltpu.make_async_remote_copy(
            src_ref=sent.at[t, block(of)],
            dst_ref=got.at[t, block(of)],
            send_sem=send_sem.at[t, of],
            recv_sem=recv_sem.at[t, of],
            device_id={"expert": of},
            device_id_type=MESH,
        )

    @pl.loop(1, n_exp)
    def _(k):
        exchange(0, k).start()

    got[0, block(me)] = sent[0, block(me)]
    weights = weights_ref[...].astype(F32)
    scaled = (weights * grads_ref[...].astype(F32)).astype(BF16)
    sent[1] = jnp.dot(place, scaled, preferred_element_type=F32).astype(BF16)

    @pl.loop(1, n_exp)
    def _(k):
        exchange(1, k).start()

    got[1, block(me)] = sent[1, block(me)]

    for load in loads:
        load.wait()

    @pl.loop(1, n_exp)
    def _(k):
        arrival(0, k).wait_recv()

    nt = (((1,), (1,)), ((), ()))

    @pl.loop(0, units // tile)
    def _(j):
        span = pl.ds(pl.multiple_of(j * tile, tile), tile)
        preact[span, :] = lax.dot_general(gate[span, :], got[0], nt, preferred_element_type=F32)

    @pl.loop(1, n_exp)
    def _(k):
        arrival(1, k).wait_recv()

    def second(j, total):
        span = pl.ds(pl.multiple_of(j * tile, tile), tile)
        slope = lax.dot_general(down[span, :], got[1], nt, preferred_element_type=F32)
        value = preact[span, :]
        sigma = jax.nn.sigmoid(value)
        hidden = (value * sigma).astype(BF16)
        hid_t[span, :] = hidden
        da_t[span, :] = (slope * (sigma * (1.0 + value * (1.0 - sigma)))).astype(BF16)
        return total + jnp.sum(hidden.astype(F32) * slope, axis=0, keepdims=True)

    route = lax.fori_loop(0, units // tile, second, jnp.zeros((1, slots), F32))

    def term(t, d, span):
        left = da_t if t == 0 else hid_t
        start = d * part if isinstance(d, int) else pl.multiple_of(d * part, part)
        return jnp.dot(
            left[pl.ds(start, part), :], got[t, :, span], preferred_element_type=F32
        )

    def columns(c):
        return pl.ds(pl.multiple_of(c * piece, piece), piece)

    def hop(buf, s_sem, r_sem, t, d, c, to):
        return pltpu.make_async_remote_copy(
            src_ref=buf.at[t, d, c],
            dst_ref=buf.at[t, d, c],
            send_sem=s_sem.at[t, d, c],
            recv_sem=r_sem.at[t, d, c],
            device_id={"dp": to},
            device_id_type=MESH,
        )

    def rightward(t, d, c, to=None):
        return hop(right_buf, r_send, r_recv, t, d - 1, c, up)

    def leftward(t, d, c, to=None):
        return hop(left_buf, l_send, l_recv, t, d, c, low)

    def pass_on(t, d, c, copy, buf, index, first):
        own = term(t, d, columns(c))

        @pl.when(first)
        def _():
            buf[t, index, c] = own.astype(BF16)

        @pl.when(jnp.logical_not(first))
        def _():
            copy.wait_recv()
            buf[t, index, c] = (own + buf[t, index, c].astype(F32)).astype(BF16)

        copy.start()

    def returning(k):
        to = peer(k)
        return pltpu.make_async_remote_copy(
            src_ref=back.at[block(to)],
            dst_ref=returned.at[block(me)],
            send_sem=back_send.at[to],
            recv_sem=back_recv.at[me],
            device_id={"expert": to},
            device_id_type=MESH,
        )

    def homecoming(k):
        of = peer(k)
        return pltpu.make_async_remote_copy(
            src_ref=back.at[block(of)],
            dst_ref=returned.at[block(of)],
            send_sem=back_send.at[of],
            recv_sem=back_recv.at[of],
            device_id={"expert": of},
            device_id_type=MESH,
        )

    def send_back():
        tn = (((0,), (0,)), ((), ()))

        @pl.loop(0, pieces)
        def _(c):
            span = columns(c)
            back[:, span] = lax.dot_general(
                da_t[...], gate[:, span], tn, preferred_element_type=F32
            ).astype(BF16)

        tall = jnp.transpose(jnp.broadcast_to(route, (LANES, slots)))
        high = tall.astype(BF16)
        rest = (tall - high.astype(F32)).astype(BF16)
        lane = lax.broadcasted_iota(jnp.int32, (slots, LANES), 1)
        back[:, pl.ds(width, LANES)] = jnp.where(
            lane < 1, high.astype(F32), rest.astype(F32)
        ).astype(BF16)

        @pl.loop(1, n_exp)
        def _(k):
            returning(k).start()

        returned[block(me), :] = back[block(me), :]

    for i in range(n_dp - 1):
        to_r, to_l = n_dp - 1 - i, i
        for t in range(2):

            @pl.loop(0, pieces)
            def _(c):
                @pl.when(r < to_r)
                def _():
                    pass_on(t, to_r, c, rightward(t, to_r, c), right_buf, to_r - 1, r == 0)

                @pl.when(r > to_l)
                def _():
                    pass_on(t, to_l, c, leftward(t, to_l, c), left_buf, to_l, r == n_dp - 1)

            if i == 0 and t == 0:
                send_back()

    @pl.loop(1, n_exp)
    def _(k):
        homecoming(k).wait_recv()

    tn = (((0,), (0,)), ((), ()))

    @pl.loop(0, pieces)
    def _(c):
        span = columns(c)
        token_out[:, span] = lax.dot_general(
            place, returned[:, span], tn, preferred_element_type=F32
        ).astype(BF16)

    pair = lax.dot_general(
        place, returned[:, pl.ds(width, LANES)], tn, preferred_element_type=F32
    )
    route_out[...] = ((pair[:, 0:1] + pair[:, 1:2]) / weights).astype(BF16)

    for t in range(2):
        out = gate_out if t == 0 else down_out

        @pl.loop(0, pieces)
        def _(c):
            span = columns(c)
            own = term(t, r, span)

            @pl.when(r == 0)
            def _():
                hop(left_buf, l_send, l_recv, t, r, c, low).wait_recv()
                out[:, span] = (own + left_buf[t, r, c].astype(F32)).astype(BF16)

            @pl.when(r == n_dp - 1)
            def _():
                hop(right_buf, r_send, r_recv, t, r - 1, c, up).wait_recv()
                out[:, span] = (own + right_buf[t, r - 1, c].astype(F32)).astype(BF16)

            @pl.when(jnp.logical_and(r > 0, r < n_dp - 1))
            def _():
                hop(left_buf, l_send, l_recv, t, r, c, low).wait_recv()
                hop(right_buf, r_send, r_recv, t, r - 1, c, up).wait_recv()
                out[:, span] = (
                    own + left_buf[t, r, c].astype(F32) + right_buf[t, r - 1, c].astype(F32)
                ).astype(BF16)

    @pl.loop(1, n_exp)
    def _(k):
        exchange(0, k).wait_send()
        exchange(1, k).wait_send()
        returning(k).wait_send()

    for i in range(n_dp - 1):
        to_r, to_l = n_dp - 1 - i, i

        @pl.loop(0, 2 * pieces)
        def _(m):
            t, c = m // pieces, lax.rem(m, pieces)

            @pl.when(r < to_r)
            def _():
                rightward(t, to_r, c).wait_send()

            @pl.when(r > to_l)
            def _():
                leftward(t, to_l, c).wait_send()


def per_device(tokens, expert_ids, route_weights, out_grad, gate_weight, down_weight):
    rows, width = tokens.shape
    n_exp, n_dp = lax.axis_size("expert"), lax.axis_size("dp")
    top = expert_ids.shape[1]
    assert top == 1
    cap = -(-max(2, 2 * rows * top // n_exp) // 16) * 16
    slots = n_exp * cap
    units = gate_weight.shape[1]
    part = units // n_dp
    pieces = max(1, width // 512)
    piece = width // pieces
    vmem = pl.BlockSpec(memory_space=pltpu.VMEM)
    hbm = pl.BlockSpec(memory_space=pl.ANY)
    token_grad, route_grad, gate_grad, down_grad = pl.pallas_call(
        functools.partial(kernel, n_dp, n_exp, cap, pieces),
        out_shape=(
            jax.ShapeDtypeStruct((rows, width), BF16),
            jax.ShapeDtypeStruct((rows, 1), BF16),
            jax.ShapeDtypeStruct((part, width), BF16),
            jax.ShapeDtypeStruct((part, width), BF16),
        ),
        in_specs=[vmem, vmem, vmem, vmem, hbm, hbm],
        out_specs=(vmem, vmem, vmem, vmem),
        scratch_shapes=[
            pltpu.VMEM((2, slots, width), BF16),
            pltpu.VMEM((2, slots, width), BF16),
            pltpu.VMEM((units, width), BF16),
            pltpu.VMEM((units, width), BF16),
            pltpu.VMEM((units, slots), F32),
            pltpu.VMEM((units, slots), BF16),
            pltpu.VMEM((units, slots), BF16),
            pltpu.VMEM((slots, width + LANES), BF16),
            pltpu.VMEM((slots, width + LANES), BF16),
            pltpu.VMEM((2, n_dp - 1, pieces, part, piece), BF16),
            pltpu.VMEM((2, n_dp - 1, pieces, part, piece), BF16),
            pltpu.SemaphoreType.DMA((2,)),
            pltpu.SemaphoreType.DMA((2, n_exp)),
            pltpu.SemaphoreType.DMA((2, n_exp)),
            pltpu.SemaphoreType.DMA((n_exp,)),
            pltpu.SemaphoreType.DMA((n_exp,)),
            pltpu.SemaphoreType.DMA((2, n_dp - 1, pieces)),
            pltpu.SemaphoreType.DMA((2, n_dp - 1, pieces)),
            pltpu.SemaphoreType.DMA((2, n_dp - 1, pieces)),
            pltpu.SemaphoreType.DMA((2, n_dp - 1, pieces)),
        ],
        compiler_params=pltpu.CompilerParams(
            collective_id=0, has_side_effects=True, vmem_limit_bytes=67_000_000
        ),
    )(
        expert_ids.reshape(1, rows), tokens, route_weights, out_grad,
        gate_weight[0], down_weight[0],
    )
    return token_grad, route_grad, gate_grad[None], down_grad[None]


def solution(mesh):
    placed = (
        P(("dp", "expert"), None),
        P(("dp", "expert"), None),
        P(("dp", "expert"), None),
        P(("dp", "expert"), None),
        P("expert", None, None),
        P("expert", None, None),
    )
    return jax.shard_map(
        per_device,
        mesh=mesh,
        in_specs=placed,
        out_specs=(
            P(("dp", "expert"), None),
            P(("dp", "expert"), None),
            P("expert", "dp", None),
            P("expert", "dp", None),
        ),
        check_vma=False,
    )
```

```python
import functools

import jax
import jax.numpy as jnp
from jax import lax
from jax.experimental import pallas as pl
from jax.experimental.pallas import tpu as pltpu
from jax.sharding import PartitionSpec as P

MESH = pl.DeviceIdType.MESH
BF16, F32 = jnp.bfloat16, jnp.float32
LANES = 128


def kernel(
    n_dp, n_exp, cap, pieces,
    ids_ref, tokens_ref, weights_ref, grads_ref, gate_hbm, down_hbm,
    token_out, route_out, gate_out, down_out,
    sent, got, gate, down, preact, hid_t, da_t, back, returned, right_buf, left_buf,
    load_sem, send_sem, recv_sem, back_send, back_recv, r_send, r_recv, l_send, l_recv,
    x_send, x_recv, g_send, g_recv, cut_send, cut_recv,
):
    rows, width = tokens_ref.shape
    slots = n_exp * cap
    units = gate.shape[0]
    part = units // n_dp
    piece = width // pieces
    tile = 256 if units % 256 == 0 else part
    r = lax.axis_index("dp")
    me = lax.axis_index("expert")

    def peer(k):
        return lax.rem(me + k, n_exp)

    def block(e):
        return pl.ds(pl.multiple_of(e * cap, cap), cap)

    loads = [
        pltpu.make_async_copy(gate_hbm, gate, load_sem.at[0]),
        pltpu.make_async_copy(down_hbm, down, load_sem.at[1]),
    ]
    for load in loads:
        load.start()

    barrier = pltpu.get_barrier_semaphore()

    @pl.loop(1, n_exp)
    def _(k):
        pl.semaphore_signal(barrier, inc=1, device_id={"expert": peer(k)}, device_id_type=MESH)

    up, low = lax.rem(r + 1, n_dp), lax.rem(r + n_dp - 1, n_dp)
    for other in (up, low):
        pl.semaphore_signal(barrier, inc=1, device_id={"dp": other}, device_id_type=MESH)

    ids = ids_ref[...]
    names = lax.broadcasted_iota(jnp.int32, (max(n_exp, 16), rows), 0)
    one_hot = (names == ids).astype(F32)
    before = (
        lax.broadcasted_iota(jnp.int32, (rows, rows), 0)
        < lax.broadcasted_iota(jnp.int32, (rows, rows), 1)
    ).astype(F32)
    counts = jnp.dot(one_hot.astype(BF16), before.astype(BF16), preferred_element_type=F32)
    rank = jnp.sum(counts * one_hot, axis=0, keepdims=True).astype(jnp.int32)
    target = ids * cap + rank
    place = (lax.broadcasted_iota(jnp.int32, (slots, rows), 0) == target).astype(F32).astype(BF16)

    sent[0] = jnp.dot(place, tokens_ref[...], preferred_element_type=F32).astype(BF16)
    pl.semaphore_wait(barrier, n_exp - 1 + 2)

    def exchange(t, k):
        to = peer(k)
        return pltpu.make_async_remote_copy(
            src_ref=sent.at[t, block(to)],
            dst_ref=got.at[t, block(me)],
            send_sem=send_sem.at[t, to],
            recv_sem=recv_sem.at[t, me],
            device_id={"expert": to},
            device_id_type=MESH,
        )

    def arrival(t, k):
        of = peer(k)
        return pltpu.make_async_remote_copy(
            src_ref=sent.at[t, block(of)],
            dst_ref=got.at[t, block(of)],
            send_sem=send_sem.at[t, of],
            recv_sem=recv_sem.at[t, of],
            device_id={"expert": of},
            device_id_type=MESH,
        )

    @pl.loop(1, n_exp)
    def _(k):
        exchange(0, k).start()

    got[0, block(me)] = sent[0, block(me)]
    weights = jnp.transpose(
        jnp.broadcast_to(weights_ref[...].astype(F32), (LANES, rows))
    )[:, 0:1]
    scaled = (weights * grads_ref[...].astype(F32)).astype(BF16)
    sent[1] = jnp.dot(place, scaled, preferred_element_type=F32).astype(BF16)

    @pl.loop(1, n_exp)
    def _(k):
        exchange(1, k).start()

    got[1, block(me)] = sent[1, block(me)]

    for load in loads:
        load.wait()

    end = jnp.logical_or(r == 0, r == n_dp - 1)
    after_end = jnp.logical_or(r == 1, r == n_dp - 2)
    inner = jnp.where(r == 0, up, low)
    lower = r < n_dp // 2

    def hand_x(e):
        return pltpu.make_async_remote_copy(
            src_ref=got.at[0, block(e)],
            dst_ref=got.at[0, pl.ds(pl.multiple_of(slots + e * cap, cap), cap)],
            send_sem=x_send.at[e],
            recv_sem=x_recv.at[e],
            device_id={"dp": inner},
            device_id_type=MESH,
        )

    def hand_g(c):
        span = pl.ds(pl.multiple_of(c * piece, piece), piece)
        return pltpu.make_async_remote_copy(
            src_ref=got.at[1, pl.ds(0, slots), span],
            dst_ref=got.at[1, pl.ds(slots, slots), span],
            send_sem=g_send.at[c],
            recv_sem=g_recv.at[c],
            device_id={"dp": inner},
            device_id_type=MESH,
        )

    def hand_cut(t, d):
        left = da_t if t == 0 else hid_t
        own = pl.ds(pl.multiple_of(d * part, part), part)
        return pltpu.make_async_remote_copy(
            src_ref=left.at[own, pl.ds(0, slots)],
            dst_ref=left.at[own, pl.ds(slots, slots)],
            send_sem=cut_send.at[t, d],
            recv_sem=cut_recv.at[t, d],
            device_id={"dp": inner},
            device_id_type=MESH,
        )

    @pl.when(end)
    def _():
        hand_x(me).start()

    @pl.loop(1, n_exp)
    def _(k):
        arrival(0, k).wait_recv()

        @pl.when(end)
        def _():
            hand_x(peer(k)).start()

    nt = (((1,), (1,)), ((), ()))

    @pl.loop(0, units // tile)
    def _(j):
        span = pl.ds(pl.multiple_of(j * tile, tile), tile)
        preact[span, :] = lax.dot_general(
            gate[span, :], got[0, 0:slots, :], nt, preferred_element_type=F32)

    @pl.loop(1, n_exp)
    def _(k):
        arrival(1, k).wait_recv()

    def second(j, total):
        span = pl.ds(pl.multiple_of(j * tile, tile), tile)
        slope = lax.dot_general(
            down[span, :], got[1, 0:slots, :], nt, preferred_element_type=F32
        )
        value = preact[span, :]
        sigma = jax.nn.sigmoid(value)
        hidden = (value * sigma).astype(BF16)
        hid_t[span, 0:slots] = hidden
        da_t[span, 0:slots] = (slope * (sigma * (1.0 + value * (1.0 - sigma)))).astype(BF16)
        return total + jnp.sum(hidden.astype(F32) * slope, axis=0, keepdims=True)

    route = lax.fori_loop(0, units // tile, second, jnp.zeros((1, slots), F32))

    @pl.when(end)
    def _():
        for t in range(2):

            @pl.loop(0, n_dp - 1)
            def _(j):
                hand_cut(t, jnp.where(r == 0, n_dp - 1 - j, j)).start()

        @pl.loop(0, pieces)
        def _(c):
            hand_g(c).start()

    def term(t, d, span, wide):
        left = da_t if t == 0 else hid_t
        start = d * part if isinstance(d, int) else pl.multiple_of(d * part, part)
        depth = 2 * slots if wide else slots
        return jnp.dot(
            left[pl.ds(start, part), 0:depth],
            got[t, 0:depth, span],
            preferred_element_type=F32,
        )

    def columns(c):
        return pl.ds(pl.multiple_of(c * piece, piece), piece)

    def hop(buf, s_sem, r_sem, t, d, c, to):
        return pltpu.make_async_remote_copy(
            src_ref=buf.at[t, d, c],
            dst_ref=buf.at[t, d, c],
            send_sem=s_sem.at[t, d, c],
            recv_sem=r_sem.at[t, d, c],
            device_id={"dp": to},
            device_id_type=MESH,
        )

    def rightward(t, d, c, to=None):
        return hop(right_buf, r_send, r_recv, t, d - 1, c, up)

    def leftward(t, d, c, to=None):
        return hop(left_buf, l_send, l_recv, t, d, c, low)

    def pass_on(t, d, c, copy, buf, index, first):
        @pl.when(first)
        def _():
            buf[t, index, c] = term(t, d, columns(c), True).astype(BF16)

        @pl.when(jnp.logical_not(first))
        def _():
            own = term(t, d, columns(c), False)
            copy.wait_recv()
            buf[t, index, c] = (own + buf[t, index, c].astype(F32)).astype(BF16)

        copy.start()

    def go_right(t):
        for d in range(n_dp - 1, 1, -1):

            @pl.when(r == 1)
            def _():
                hand_cut(t, d).wait_recv()

            @pl.when(jnp.logical_and(r > 0, r < d))
            def _():
                @pl.loop(0, pieces)
                def _(c):
                    if t == 1 and d == n_dp - 1:

                        @pl.when(r == 1)
                        def _():
                            hand_g(c).wait_recv()

                    pass_on(t, d, c, rightward(t, d, c), right_buf, d - 1, r == 1)

    def go_left(t):
        for d in range(n_dp - 2):

            @pl.when(r == n_dp - 2)
            def _():
                hand_cut(t, d).wait_recv()

            @pl.when(jnp.logical_and(r < n_dp - 1, r > d))
            def _():
                @pl.loop(0, pieces)
                def _(c):
                    if t == 1 and d == 0:

                        @pl.when(r == n_dp - 2)
                        def _():
                            hand_g(c).wait_recv()

                    pass_on(t, d, c, leftward(t, d, c), left_buf, d, r == n_dp - 2)

    def returning(k):
        to = peer(k)
        return pltpu.make_async_remote_copy(
            src_ref=back.at[block(to)],
            dst_ref=returned.at[block(me)],
            send_sem=back_send.at[to],
            recv_sem=back_recv.at[me],
            device_id={"expert": to},
            device_id_type=MESH,
        )

    def homecoming(k):
        of = peer(k)
        return pltpu.make_async_remote_copy(
            src_ref=back.at[block(of)],
            dst_ref=returned.at[block(of)],
            send_sem=back_send.at[of],
            recv_sem=back_recv.at[of],
            device_id={"expert": of},
            device_id_type=MESH,
        )

    def send_back():
        tn = (((0,), (0,)), ((), ()))

        @pl.loop(0, pieces)
        def _(c):
            span = columns(c)
            back[:, span] = lax.dot_general(
                da_t[:, 0:slots], gate[:, span], tn, preferred_element_type=F32
            ).astype(BF16)

        tall = jnp.transpose(jnp.broadcast_to(route, (LANES, slots)))
        high = tall.astype(BF16)
        rest = (tall - high.astype(F32)).astype(BF16)
        lane = lax.broadcasted_iota(jnp.int32, (slots, LANES), 1)
        back[:, pl.ds(width, LANES)] = jnp.where(
            lane < 1, high.astype(F32), rest.astype(F32)
        ).astype(BF16)

        @pl.loop(1, n_exp)
        def _(k):
            returning(k).start()

        returned[block(me), :] = back[block(me), :]

    send_back()

    @pl.when(after_end)
    def _():
        @pl.loop(0, n_exp)
        def _(e):
            hand_x(e).wait_recv()

    for t in range(2):

        @pl.when(lower)
        def _():
            go_right(t)

        go_left(t)

        @pl.when(jnp.logical_not(lower))
        def _():
            go_right(t)

    @pl.loop(1, n_exp)
    def _(k):
        homecoming(k).wait_recv()

    tn = (((0,), (0,)), ((), ()))

    @pl.loop(0, pieces)
    def _(c):
        span = columns(c)
        token_out[:, span] = lax.dot_general(
            place, returned[:, span], tn, preferred_element_type=F32
        ).astype(BF16)

    pair = lax.dot_general(
        place, returned[:, pl.ds(width, LANES)], tn, preferred_element_type=F32
    )
    total = jnp.broadcast_to((pair[:, 0:1] + pair[:, 1:2]) / weights, (rows, LANES))
    route_out[...] = jnp.transpose(total)[0:1, :].astype(BF16)

    for t in range(2):
        out = gate_out if t == 0 else down_out

        @pl.when(after_end)
        def _():
            hand_cut(t, r).wait_recv()

        @pl.loop(0, pieces)
        def _(c):
            span = columns(c)

            def from_right():
                hop(left_buf, l_send, l_recv, t, r, c, low).wait_recv()
                return left_buf[t, r, c].astype(F32)

            def from_left():
                hop(right_buf, r_send, r_recv, t, r - 1, c, up).wait_recv()
                return right_buf[t, r - 1, c].astype(F32)

            @pl.when(r == 0)
            def _():
                out[:, span] = (term(t, r, span, False) + from_right()).astype(BF16)

            @pl.when(r == n_dp - 1)
            def _():
                out[:, span] = (term(t, r, span, False) + from_left()).astype(BF16)

            @pl.when(r == 1)
            def _():
                out[:, span] = (term(t, r, span, True) + from_right()).astype(BF16)

            @pl.when(r == n_dp - 2)
            def _():
                out[:, span] = (term(t, r, span, True) + from_left()).astype(BF16)

            @pl.when(jnp.logical_and(r > 1, r < n_dp - 2))
            def _():
                out[:, span] = (term(t, r, span, False) + from_right() + from_left()).astype(BF16)

    @pl.loop(1, n_exp)
    def _(k):
        exchange(0, k).wait_send()
        exchange(1, k).wait_send()
        returning(k).wait_send()

    @pl.when(end)
    def _():
        @pl.loop(0, n_exp)
        def _(e):
            hand_x(e).wait_send()

        @pl.loop(0, pieces)
        def _(c):
            hand_g(c).wait_send()

        for t in range(2):

            @pl.loop(0, n_dp - 1)
            def _(j):
                hand_cut(t, jnp.where(r == 0, n_dp - 1 - j, j)).wait_send()

    for t in range(2):
        for d in range(n_dp):

            @pl.loop(0, pieces)
            def _(c):
                if d > 1:

                    @pl.when(jnp.logical_and(r > 0, r < d))
                    def _():
                        rightward(t, d, c).wait_send()

                if d < n_dp - 2:

                    @pl.when(jnp.logical_and(r < n_dp - 1, r > d))
                    def _():
                        leftward(t, d, c).wait_send()


def settle(*refs):
    half = len(refs) // 2
    for source, out in zip(refs[:half], refs[half:]):
        out[...] = source[...]


def per_device(tokens, expert_ids, route_weights, out_grad, gate_weight, down_weight):
    rows, width = tokens.shape
    n_exp, n_dp = lax.axis_size("expert"), lax.axis_size("dp")
    top = expert_ids.shape[1]
    assert top == 1 and n_dp >= 4
    cap = -(-max(2, 2 * rows * top // n_exp) // 16) * 16
    slots = n_exp * cap
    units = gate_weight.shape[1]
    part = units // n_dp
    pieces = max(1, width // 512)
    piece = width // pieces
    vmem = pl.BlockSpec(memory_space=pltpu.VMEM)
    hbm = pl.BlockSpec(memory_space=pl.ANY)
    results = pl.pallas_call(
        functools.partial(kernel, n_dp, n_exp, cap, pieces),
        out_shape=(
            jax.ShapeDtypeStruct((rows, width), BF16),
            jax.ShapeDtypeStruct((1, rows), BF16),
            jax.ShapeDtypeStruct((part, width), BF16),
            jax.ShapeDtypeStruct((part, width), BF16),
        ),
        in_specs=[vmem, vmem, vmem, vmem, hbm, hbm],
        out_specs=(vmem, vmem, vmem, vmem),
        scratch_shapes=[
            pltpu.VMEM((2, slots, width), BF16),
            pltpu.VMEM((2, 2 * slots, width), BF16),
            pltpu.VMEM((units, width), BF16),
            pltpu.VMEM((units, width), BF16),
            pltpu.VMEM((units, slots), F32),
            pltpu.VMEM((units, 2 * slots), BF16),
            pltpu.VMEM((units, 2 * slots), BF16),
            pltpu.VMEM((slots, width + LANES), BF16),
            pltpu.VMEM((slots, width + LANES), BF16),
            pltpu.VMEM((2, n_dp - 1, pieces, part, piece), BF16),
            pltpu.VMEM((2, n_dp - 1, pieces, part, piece), BF16),
            pltpu.SemaphoreType.DMA((2,)),
            pltpu.SemaphoreType.DMA((2, n_exp)),
            pltpu.SemaphoreType.DMA((2, n_exp)),
            pltpu.SemaphoreType.DMA((n_exp,)),
            pltpu.SemaphoreType.DMA((n_exp,)),
            pltpu.SemaphoreType.DMA((2, n_dp - 1, pieces)),
            pltpu.SemaphoreType.DMA((2, n_dp - 1, pieces)),
            pltpu.SemaphoreType.DMA((2, n_dp - 1, pieces)),
            pltpu.SemaphoreType.DMA((2, n_dp - 1, pieces)),
            pltpu.SemaphoreType.DMA((n_exp,)),
            pltpu.SemaphoreType.DMA((n_exp,)),
            pltpu.SemaphoreType.DMA((pieces,)),
            pltpu.SemaphoreType.DMA((pieces,)),
            pltpu.SemaphoreType.DMA((2, n_dp)),
            pltpu.SemaphoreType.DMA((2, n_dp)),
        ],
        compiler_params=pltpu.CompilerParams(
            collective_id=0, has_side_effects=True, vmem_limit_bytes=67_000_000
        ),
    )(
        expert_ids.reshape(1, rows), tokens, route_weights.reshape(1, rows), out_grad,
        gate_weight[0], down_weight[0],
    )
    token_grad, route_grad, gate_grad, down_grad = pl.pallas_call(
        settle,
        out_shape=tuple(jax.ShapeDtypeStruct(a.shape, a.dtype) for a in results),
        in_specs=[vmem] * 4,
        out_specs=(vmem,) * 4,
    )(*results)
    return token_grad, route_grad.reshape(rows, 1), gate_grad[None], down_grad[None]


def solution(mesh):
    placed = (
        P(("dp", "expert"), None),
        P(("dp", "expert"), None),
        P(("dp", "expert"), None),
        P(("dp", "expert"), None),
        P("expert", None, None),
        P("expert", None, None),
    )
    return jax.shard_map(
        per_device,
        mesh=mesh,
        in_specs=placed,
        out_specs=(
            P(("dp", "expert"), None),
            P(("dp", "expert"), None),
            P("expert", "dp", None),
            P("expert", "dp", None),
        ),
        check_vma=False,
    )
```

```python
import functools

import jax
import jax.numpy as jnp
from jax import lax
from jax.experimental import pallas as pl
from jax.experimental.pallas import tpu as pltpu
from jax.sharding import PartitionSpec as P

MESH = pl.DeviceIdType.MESH
BF16, F32 = jnp.bfloat16, jnp.float32
LANES = 128


def kernel(
    n_dp, n_exp, cap, pieces,
    ids_ref, tokens_ref, weights_ref, grads_ref, gate_hbm, down_hbm,
    token_out, route_out, gate_out, down_out,
    sent, got, gate, down, preact, hid_t, da_t, back, returned, right_buf, left_buf,
    load_sem, send_sem, recv_sem, back_send, back_recv, r_send, r_recv, l_send, l_recv,
    x_send, x_recv, g_send, g_recv, cut_send, cut_recv,
    raw, raw_ids, far_sent, pair_out, pair_in,
    raw_send, raw_recv, far_send, far_recv, slice_send, slice_recv, pair_send, pair_recv,
):
    rows, width = tokens_ref.shape
    slots = n_exp * cap
    units = gate.shape[0]
    part = units // n_dp
    piece = width // pieces
    tile = 256 if units % 256 == 0 else part
    r = lax.axis_index("dp")
    me = lax.axis_index("expert")

    def peer(k):
        return lax.rem(me + k, n_exp)

    def block(e):
        return pl.ds(pl.multiple_of(e * cap, cap), cap)

    loads = [
        pltpu.make_async_copy(gate_hbm, gate, load_sem.at[0]),
        pltpu.make_async_copy(down_hbm, down, load_sem.at[1]),
    ]
    for load in loads:
        load.start()

    barrier = pltpu.get_barrier_semaphore()

    @pl.loop(1, n_exp)
    def _(k):
        pl.semaphore_signal(barrier, inc=1, device_id={"expert": peer(k)}, device_id_type=MESH)

    up, low = lax.rem(r + 1, n_dp), lax.rem(r + n_dp - 1, n_dp)
    deep = n_dp == 4

    @pl.loop(1, n_dp)
    def _(k):
        other = lax.rem(r + k, n_dp)
        pl.semaphore_signal(barrier, inc=1, device_id={"dp": other}, device_id_type=MESH)

    def placement(ids):
        names = lax.broadcasted_iota(jnp.int32, (max(n_exp, 16), rows), 0)
        one_hot = (names == ids).astype(F32)
        before = (
            lax.broadcasted_iota(jnp.int32, (rows, rows), 0)
            < lax.broadcasted_iota(jnp.int32, (rows, rows), 1)
        ).astype(F32)
        counts = jnp.dot(one_hot.astype(BF16), before.astype(BF16), preferred_element_type=F32)
        rank = jnp.sum(counts * one_hot, axis=0, keepdims=True).astype(jnp.int32)
        target = ids * cap + rank
        match = lax.broadcasted_iota(jnp.int32, (slots, rows), 0) == target
        return match.astype(F32).astype(BF16)

    place = placement(ids_ref[...])
    is_end = jnp.logical_or(r == 0, r == n_dp - 1)
    which = jnp.where(is_end, 0, 1)
    across = jnp.where(r < 2, 2, 1)

    def raw_copies(j):
        return [
            pltpu.make_async_remote_copy(
                src_ref=source, dst_ref=held.at[j],
                send_sem=raw_send.at[i], recv_sem=raw_recv.at[i, j],
                device_id={"dp": across}, device_id_type=MESH,
            )
            for i, (source, held) in enumerate(((ids_ref, raw_ids), (tokens_ref, raw)))
        ]

    def far_block(j, e):
        return pl.ds(pl.multiple_of((1 + j) * slots + e * cap, cap), cap)

    def far_exchange(j, to, at, peer_id=None):
        return pltpu.make_async_remote_copy(
            src_ref=far_sent.at[j, block(to)],
            dst_ref=got.at[0, far_block(j, at)],
            send_sem=far_send.at[j, to],
            recv_sem=far_recv.at[j, at],
            device_id={"expert": to if peer_id is None else peer_id},
            device_id_type=MESH,
        )

    def slice_copy(j):
        own = pl.ds(pl.multiple_of(jnp.where(r < 2, 2 * part, 0), part), 2 * part)
        return pltpu.make_async_remote_copy(
            src_ref=da_t.at[own, pl.ds(0, slots)],
            dst_ref=da_t.at[own, pl.ds(pl.multiple_of((1 + j) * slots, slots), slots)],
            send_sem=slice_send,
            recv_sem=slice_recv.at[j],
            device_id={"dp": across},
            device_id_type=MESH,
        )

    def slice_wait(j):
        own = pl.ds(pl.multiple_of(jnp.where(r < 2, 0, 2 * part), part), 2 * part)
        far = pl.ds(pl.multiple_of((1 + j) * slots, slots), slots)
        return pltpu.make_async_remote_copy(
            src_ref=da_t.at[own, pl.ds(0, slots)],
            dst_ref=da_t.at[own, far],
            send_sem=slice_send,
            recv_sem=slice_recv.at[j],
            device_id={"dp": across},
            device_id_type=MESH,
        )

    partner = r + 1 - 2 * lax.rem(r, 2)

    def pair_copy(c):
        return pltpu.make_async_remote_copy(
            src_ref=pair_out.at[c], dst_ref=pair_in.at[c],
            send_sem=pair_send.at[c], recv_sem=pair_recv.at[c],
            device_id={"dp": partner}, device_id_type=MESH,
        )

    sent[0] = jnp.dot(place, tokens_ref[...], preferred_element_type=F32).astype(BF16)
    pl.semaphore_wait(barrier, n_exp - 1 + n_dp - 1)

    def exchange(t, k):
        to = peer(k)
        return pltpu.make_async_remote_copy(
            src_ref=sent.at[t, block(to)],
            dst_ref=got.at[t, block(me)],
            send_sem=send_sem.at[t, to],
            recv_sem=recv_sem.at[t, me],
            device_id={"expert": to},
            device_id_type=MESH,
        )

    def arrival(t, k):
        of = peer(k)
        return pltpu.make_async_remote_copy(
            src_ref=sent.at[t, block(of)],
            dst_ref=got.at[t, block(of)],
            send_sem=send_sem.at[t, of],
            recv_sem=recv_sem.at[t, of],
            device_id={"expert": of},
            device_id_type=MESH,
        )

    @pl.loop(1, n_exp)
    def _(k):
        exchange(0, k).start()

    if deep:
        for copy in raw_copies(which):
            copy.start()

    got[0, block(me)] = sent[0, block(me)]
    weights = jnp.transpose(
        jnp.broadcast_to(weights_ref[...].astype(F32), (LANES, rows))
    )[:, 0:1]
    scaled = (weights * grads_ref[...].astype(F32)).astype(BF16)
    sent[1] = jnp.dot(place, scaled, preferred_element_type=F32).astype(BF16)

    @pl.loop(1, n_exp)
    def _(k):
        exchange(1, k).start()

    got[1, block(me)] = sent[1, block(me)]

    for load in loads:
        load.wait()

    end = jnp.logical_or(r == 0, r == n_dp - 1)
    after_end = jnp.logical_or(r == 1, r == n_dp - 2)
    inner = jnp.where(r == 0, up, low)
    lower = r < n_dp // 2

    def hand_x(e):
        return pltpu.make_async_remote_copy(
            src_ref=got.at[first, block(e)],
            dst_ref=got.at[first, pl.ds(pl.multiple_of(slots + e * cap, cap), cap)],
            send_sem=x_send.at[e],
            recv_sem=x_recv.at[e],
            device_id={"dp": inner},
            device_id_type=MESH,
        )

    def hand_g(c):
        span = pl.ds(pl.multiple_of(c * piece, piece), piece)
        return pltpu.make_async_remote_copy(
            src_ref=got.at[1, pl.ds(0, slots), span],
            dst_ref=got.at[1, pl.ds(slots, slots), span],
            send_sem=g_send.at[c],
            recv_sem=g_recv.at[c],
            device_id={"dp": inner},
            device_id_type=MESH,
        )

    def hand_cut(t, d):
        left = da_t if t == 0 else hid_t
        own = pl.ds(pl.multiple_of(d * part, part), part)
        return pltpu.make_async_remote_copy(
            src_ref=left.at[own, pl.ds(0, slots)],
            dst_ref=left.at[own, pl.ds(slots, slots)],
            send_sem=cut_send.at[t, d],
            recv_sem=cut_recv.at[t, d],
            device_id={"dp": inner},
            device_id_type=MESH,
        )

    first = 1 if deep else 0

    @pl.when(end)
    def _():
        hand_x(me).start()

    @pl.loop(1, n_exp)
    def _(k):
        arrival(0, k).wait_recv()

        if not deep:

            @pl.when(end)
            def _():
                hand_x(peer(k)).start()

    nt = (((1,), (1,)), ((), ()))

    @pl.loop(0, units // tile)
    def _(j):
        span = pl.ds(pl.multiple_of(j * tile, tile), tile)
        value = lax.dot_general(
            gate[span, :], got[0, 0:slots, :], nt, preferred_element_type=F32
        )
        preact[span, :] = value
        hid_t[span, 0:slots] = (value * jax.nn.sigmoid(value)).astype(BF16)

    def hand_cuts(t):
        @pl.when(end)
        def _():
            @pl.loop(0, n_dp - 1)
            def _(j):
                hand_cut(t, jnp.where(r == 0, n_dp - 1 - j, j)).start()

    if deep:
        hand_cuts(1)

    @pl.loop(1, n_exp)
    def _(k):
        arrival(1, k).wait_recv()

        if deep:

            @pl.when(end)
            def _():
                hand_x(peer(k)).start()

    def second(j, total):
        span = pl.ds(pl.multiple_of(j * tile, tile), tile)
        slope = lax.dot_general(
            down[span, :], got[1, 0:slots, :], nt, preferred_element_type=F32
        )
        value = preact[span, :]
        sigma = jax.nn.sigmoid(value)
        da_t[span, 0:slots] = (slope * (sigma * (1.0 + value * (1.0 - sigma)))).astype(BF16)
        return total + jnp.sum(hid_t[span, 0:slots].astype(F32) * slope, axis=0, keepdims=True)

    route = lax.fori_loop(0, units // tile, second, jnp.zeros((1, slots), F32))

    if deep:
        slice_copy(which).start()

        @pl.when(after_end)
        def _():
            for j in (1, 0):
                for copy in raw_copies(j):
                    copy.wait_recv()
                far_sent[j] = jnp.dot(
                    placement(raw_ids[j]), raw[j], preferred_element_type=F32
                ).astype(BF16)

                @pl.loop(1, n_exp)
                def _(k):
                    far_exchange(j, peer(k), me).start()

                got[0, far_block(j, me)] = far_sent[j, block(me)]
    else:
        hand_cuts(0)
        hand_cuts(1)

        @pl.when(end)
        def _():
            @pl.loop(0, pieces)
            def _(c):
                hand_g(c).start()

    def term(t, d, span, wide):
        left = da_t if t == 0 else hid_t
        start = d * part if isinstance(d, int) else pl.multiple_of(d * part, part)
        depth = (3 if deep and t == 0 else 2) * slots if wide else slots
        return jnp.dot(
            left[pl.ds(start, part), 0:depth],
            got[t, 0:depth, span],
            preferred_element_type=F32,
        )

    def columns(c):
        return pl.ds(pl.multiple_of(c * piece, piece), piece)

    def hop(buf, s_sem, r_sem, t, d, c, to):
        return pltpu.make_async_remote_copy(
            src_ref=buf.at[t, d, c],
            dst_ref=buf.at[t, d, c],
            send_sem=s_sem.at[t, d, c],
            recv_sem=r_sem.at[t, d, c],
            device_id={"dp": to},
            device_id_type=MESH,
        )

    def rightward(t, d, c, to=None):
        return hop(right_buf, r_send, r_recv, t, d - 1, c, up)

    def leftward(t, d, c, to=None):
        return hop(left_buf, l_send, l_recv, t, d, c, low)

    def pass_on(t, d, c, copy, buf, index, first):
        @pl.when(first)
        def _():
            buf[t, index, c] = term(t, d, columns(c), True).astype(BF16)

        @pl.when(jnp.logical_not(first))
        def _():
            own = term(t, d, columns(c), False)
            copy.wait_recv()
            buf[t, index, c] = (own + buf[t, index, c].astype(F32)).astype(BF16)

        copy.start()

    def go_right(t):
        for d in range(n_dp - 1, 1, -1):

            @pl.when(r == 1)
            def _():
                hand_cut(t, d).wait_recv()

            @pl.when(jnp.logical_and(r > 0, r < d))
            def _():
                @pl.loop(0, pieces)
                def _(c):
                    if not deep and t == 1 and d == n_dp - 1:

                        @pl.when(r == 1)
                        def _():
                            hand_g(c).wait_recv()

                    pass_on(t, d, c, rightward(t, d, c), right_buf, d - 1, r == 1)

    def go_left(t):
        for d in range(n_dp - 2):

            @pl.when(r == n_dp - 2)
            def _():
                hand_cut(t, d).wait_recv()

            @pl.when(jnp.logical_and(r < n_dp - 1, r > d))
            def _():
                @pl.loop(0, pieces)
                def _(c):
                    if not deep and t == 1 and d == 0:

                        @pl.when(r == n_dp - 2)
                        def _():
                            hand_g(c).wait_recv()

                    pass_on(t, d, c, leftward(t, d, c), left_buf, d, r == n_dp - 2)

    def returning(k):
        to = peer(k)
        return pltpu.make_async_remote_copy(
            src_ref=back.at[block(to)],
            dst_ref=returned.at[block(me)],
            send_sem=back_send.at[to],
            recv_sem=back_recv.at[me],
            device_id={"expert": to},
            device_id_type=MESH,
        )

    def homecoming(k):
        of = peer(k)
        return pltpu.make_async_remote_copy(
            src_ref=back.at[block(of)],
            dst_ref=returned.at[block(of)],
            send_sem=back_send.at[of],
            recv_sem=back_recv.at[of],
            device_id={"expert": of},
            device_id_type=MESH,
        )

    def send_back():
        tn = (((0,), (0,)), ((), ()))

        @pl.loop(0, pieces)
        def _(c):
            span = columns(c)
            back[:, span] = lax.dot_general(
                da_t[:, 0:slots], gate[:, span], tn, preferred_element_type=F32
            ).astype(BF16)

        tall = jnp.transpose(jnp.broadcast_to(route, (LANES, slots)))
        high = tall.astype(BF16)
        rest = (tall - high.astype(F32)).astype(BF16)
        lane = lax.broadcasted_iota(jnp.int32, (slots, LANES), 1)
        back[:, pl.ds(width, LANES)] = jnp.where(
            lane < 1, high.astype(F32), rest.astype(F32)
        ).astype(BF16)

        @pl.loop(1, n_exp)
        def _(k):
            returning(k).start()

        returned[block(me), :] = back[block(me), :]

    send_back()

    @pl.when(after_end)
    def _():
        @pl.loop(0, n_exp)
        def _(e):
            hand_x(e).wait_recv()

    for t in range(first, 2):

        @pl.when(lower)
        def _():
            go_right(t)

        go_left(t)

        @pl.when(jnp.logical_not(lower))
        def _():
            go_right(t)

    if deep:

        @pl.when(after_end)
        def _():
            for j in (1, 0):
                slice_wait(j).wait_recv()

                @pl.loop(1, n_exp)
                def _(k):
                    far_exchange(j, me, peer(k), peer(k)).wait_recv()

        @pl.loop(0, pieces)
        def _(c):
            for wide, role in ((True, after_end), (False, end)):

                @pl.when(role)
                def _():
                    pair_out[c] = term(0, partner, columns(c), wide).astype(BF16)

            pair_copy(c).start()

    @pl.loop(1, n_exp)
    def _(k):
        homecoming(k).wait_recv()

    tn = (((0,), (0,)), ((), ()))

    @pl.loop(0, pieces)
    def _(c):
        span = columns(c)
        token_out[:, span] = lax.dot_general(
            place, returned[:, span], tn, preferred_element_type=F32
        ).astype(BF16)

    pair = lax.dot_general(
        place, returned[:, pl.ds(width, LANES)], tn, preferred_element_type=F32
    )
    total = jnp.broadcast_to((pair[:, 0:1] + pair[:, 1:2]) / weights, (rows, LANES))
    route_out[...] = jnp.transpose(total)[0:1, :].astype(BF16)

    if deep:

        @pl.loop(0, pieces)
        def _(c):
            span = columns(c)
            for wide, role in ((True, after_end), (False, end)):

                @pl.when(role)
                def _():
                    own = term(0, r, span, wide)
                    pair_copy(c).wait_recv()
                    gate_out[:, span] = (own + pair_in[c].astype(F32)).astype(BF16)

    for t in range(first, 2):
        out = gate_out if t == 0 else down_out

        @pl.when(after_end)
        def _():
            hand_cut(t, r).wait_recv()

        @pl.loop(0, pieces)
        def _(c):
            span = columns(c)

            def from_right():
                hop(left_buf, l_send, l_recv, t, r, c, low).wait_recv()
                return left_buf[t, r, c].astype(F32)

            def from_left():
                hop(right_buf, r_send, r_recv, t, r - 1, c, up).wait_recv()
                return right_buf[t, r - 1, c].astype(F32)

            @pl.when(r == 0)
            def _():
                out[:, span] = (term(t, r, span, False) + from_right()).astype(BF16)

            @pl.when(r == n_dp - 1)
            def _():
                out[:, span] = (term(t, r, span, False) + from_left()).astype(BF16)

            @pl.when(r == 1)
            def _():
                out[:, span] = (term(t, r, span, True) + from_right()).astype(BF16)

            @pl.when(r == n_dp - 2)
            def _():
                out[:, span] = (term(t, r, span, True) + from_left()).astype(BF16)

            @pl.when(jnp.logical_and(r > 1, r < n_dp - 2))
            def _():
                out[:, span] = (term(t, r, span, False) + from_right() + from_left()).astype(BF16)

    @pl.loop(1, n_exp)
    def _(k):
        exchange(0, k).wait_send()
        exchange(1, k).wait_send()
        returning(k).wait_send()

    @pl.when(end)
    def _():
        @pl.loop(0, n_exp)
        def _(e):
            hand_x(e).wait_send()

        if not deep:

            @pl.loop(0, pieces)
            def _(c):
                hand_g(c).wait_send()

        for t in range(first, 2):

            @pl.loop(0, n_dp - 1)
            def _(j):
                hand_cut(t, jnp.where(r == 0, n_dp - 1 - j, j)).wait_send()

    if deep:
        for copy in raw_copies(which):
            copy.wait_send()
        slice_copy(which).wait_send()

        @pl.loop(0, pieces)
        def _(c):
            pair_copy(c).wait_send()

        @pl.when(after_end)
        def _():
            for j in (1, 0):

                @pl.loop(1, n_exp)
                def _(k):
                    far_exchange(j, peer(k), me).wait_send()

    for t in range(first, 2):
        for d in range(n_dp):

            @pl.loop(0, pieces)
            def _(c):
                if d > 1:

                    @pl.when(jnp.logical_and(r > 0, r < d))
                    def _():
                        rightward(t, d, c).wait_send()

                if d < n_dp - 2:

                    @pl.when(jnp.logical_and(r < n_dp - 1, r > d))
                    def _():
                        leftward(t, d, c).wait_send()


def settle(*refs):
    half = len(refs) // 2
    for source, out in zip(refs[:half], refs[half:]):
        out[...] = source[...]


def per_device(tokens, expert_ids, route_weights, out_grad, gate_weight, down_weight):
    rows, width = tokens.shape
    n_exp, n_dp = lax.axis_size("expert"), lax.axis_size("dp")
    top = expert_ids.shape[1]
    assert top == 1 and n_dp >= 4
    cap = -(-max(2, 2 * rows * top // n_exp) // 16) * 16
    slots = n_exp * cap
    units = gate_weight.shape[1]
    part = units // n_dp
    pieces = max(1, width // 512)
    piece = width // pieces
    deep = n_dp == 4
    copies = 3 if deep else 2
    vmem = pl.BlockSpec(memory_space=pltpu.VMEM)
    hbm = pl.BlockSpec(memory_space=pl.ANY)
    results = pl.pallas_call(
        functools.partial(kernel, n_dp, n_exp, cap, pieces),
        out_shape=(
            jax.ShapeDtypeStruct((rows, width), BF16),
            jax.ShapeDtypeStruct((1, rows), BF16),
            jax.ShapeDtypeStruct((part, width), BF16),
            jax.ShapeDtypeStruct((part, width), BF16),
        ),
        in_specs=[vmem, vmem, vmem, vmem, hbm, hbm],
        out_specs=(vmem, vmem, vmem, vmem),
        scratch_shapes=[
            pltpu.VMEM((2, slots, width), BF16),
            pltpu.VMEM((2, copies * slots, width), BF16),
            pltpu.VMEM((units, width), BF16),
            pltpu.VMEM((units, width), BF16),
            pltpu.VMEM((units, slots), F32),
            pltpu.VMEM((units, copies * slots), BF16),
            pltpu.VMEM((units, copies * slots), BF16),
            pltpu.VMEM((slots, width + LANES), BF16),
            pltpu.VMEM((slots, width + LANES), BF16),
            pltpu.VMEM((2, n_dp - 1, pieces, part, piece), BF16),
            pltpu.VMEM((2, n_dp - 1, pieces, part, piece), BF16),
            pltpu.SemaphoreType.DMA((2,)),
            pltpu.SemaphoreType.DMA((2, n_exp)),
            pltpu.SemaphoreType.DMA((2, n_exp)),
            pltpu.SemaphoreType.DMA((n_exp,)),
            pltpu.SemaphoreType.DMA((n_exp,)),
            pltpu.SemaphoreType.DMA((2, n_dp - 1, pieces)),
            pltpu.SemaphoreType.DMA((2, n_dp - 1, pieces)),
            pltpu.SemaphoreType.DMA((2, n_dp - 1, pieces)),
            pltpu.SemaphoreType.DMA((2, n_dp - 1, pieces)),
            pltpu.SemaphoreType.DMA((n_exp,)),
            pltpu.SemaphoreType.DMA((n_exp,)),
            pltpu.SemaphoreType.DMA((pieces,)),
            pltpu.SemaphoreType.DMA((pieces,)),
            pltpu.SemaphoreType.DMA((2, n_dp)),
            pltpu.SemaphoreType.DMA((2, n_dp)),
            pltpu.VMEM((2, rows, width) if deep else (2, 16, LANES), BF16),
            pltpu.VMEM((2, 1, rows), jnp.int32),
            pltpu.VMEM((2, slots, width) if deep else (2, 16, LANES), BF16),
            pltpu.VMEM((pieces, part, piece) if deep else (1, 16, LANES), BF16),
            pltpu.VMEM((pieces, part, piece) if deep else (1, 16, LANES), BF16),
            pltpu.SemaphoreType.DMA((2,)),
            pltpu.SemaphoreType.DMA((2, 2)),
            pltpu.SemaphoreType.DMA((2, n_exp)),
            pltpu.SemaphoreType.DMA((2, n_exp)),
            pltpu.SemaphoreType.DMA,
            pltpu.SemaphoreType.DMA((2,)),
            pltpu.SemaphoreType.DMA((pieces,)),
            pltpu.SemaphoreType.DMA((pieces,)),
        ],
        compiler_params=pltpu.CompilerParams(
            collective_id=0, has_side_effects=True, vmem_limit_bytes=67_000_000
        ),
    )(
        expert_ids.reshape(1, rows), tokens, route_weights.reshape(1, rows), out_grad,
        gate_weight[0], down_weight[0],
    )
    token_grad, route_grad, gate_grad, down_grad = pl.pallas_call(
        settle,
        out_shape=tuple(jax.ShapeDtypeStruct(a.shape, a.dtype) for a in results),
        in_specs=[vmem] * 4,
        out_specs=(vmem,) * 4,
    )(*results)
    return token_grad, route_grad.reshape(rows, 1), gate_grad[None], down_grad[None]


def solution(mesh):
    placed = (
        P(("dp", "expert"), None),
        P(("dp", "expert"), None),
        P(("dp", "expert"), None),
        P(("dp", "expert"), None),
        P("expert", None, None),
        P("expert", None, None),
    )
    return jax.shard_map(
        per_device,
        mesh=mesh,
        in_specs=placed,
        out_specs=(
            P(("dp", "expert"), None),
            P(("dp", "expert"), None),
            P("expert", "dp", None),
            P("expert", "dp", None),
        ),
        check_vma=False,
    )
```

```python
import functools

import jax
import jax.numpy as jnp
from jax import lax
from jax.experimental import pallas as pl
from jax.experimental.pallas import tpu as pltpu
from jax.sharding import PartitionSpec as P

MESH = pl.DeviceIdType.MESH
BF16, F32 = jnp.bfloat16, jnp.float32
LANES = 128


def kernel(
    n_dp, n_exp, cap, pieces,
    ids_ref, tokens_ref, weights_ref, grads_ref, gate_hbm, down_hbm,
    token_out, route_out, gate_out, down_out,
    sent, got, gate, down, preact, hid_t, da_t, back, returned, right_buf, left_buf,
    load_sem, send_sem, recv_sem, back_send, back_recv, r_send, r_recv, l_send, l_recv,
    x_send, x_recv, g_send, g_recv, cut_send, cut_recv,
    raw, raw_ids, far_sent, pair_out, pair_in,
    raw_send, raw_recv, far_send, far_recv, slice_send, slice_recv, pair_send, pair_recv,
):
    rows, width = tokens_ref.shape
    slots = n_exp * cap
    units = gate.shape[0]
    part = units // n_dp
    piece = width // pieces
    tile = 256 if units % 256 == 0 else part
    r = lax.axis_index("dp")
    me = lax.axis_index("expert")

    def peer(k):
        return lax.rem(me + k, n_exp)

    def block(e):
        return pl.ds(pl.multiple_of(e * cap, cap), cap)

    loads = [
        pltpu.make_async_copy(gate_hbm, gate, load_sem.at[0]),
        pltpu.make_async_copy(down_hbm, down, load_sem.at[1]),
    ]
    for load in loads:
        load.start()

    barrier = pltpu.get_barrier_semaphore()

    @pl.loop(1, n_exp)
    def _(k):
        pl.semaphore_signal(barrier, inc=1, device_id={"expert": peer(k)}, device_id_type=MESH)

    up, low = lax.rem(r + 1, n_dp), lax.rem(r + n_dp - 1, n_dp)
    deep = n_dp == 4

    @pl.loop(1, n_dp)
    def _(k):
        other = lax.rem(r + k, n_dp)
        pl.semaphore_signal(barrier, inc=1, device_id={"dp": other}, device_id_type=MESH)

    def placement(ids):
        names = lax.broadcasted_iota(jnp.int32, (max(n_exp, 16), rows), 0)
        one_hot = (names == ids).astype(F32)
        before = (
            lax.broadcasted_iota(jnp.int32, (rows, rows), 0)
            < lax.broadcasted_iota(jnp.int32, (rows, rows), 1)
        ).astype(F32)
        counts = jnp.dot(one_hot.astype(BF16), before.astype(BF16), preferred_element_type=F32)
        rank = jnp.sum(counts * one_hot, axis=0, keepdims=True).astype(jnp.int32)
        target = ids * cap + rank
        match = lax.broadcasted_iota(jnp.int32, (slots, rows), 0) == target
        return match.astype(F32).astype(BF16)

    place = placement(ids_ref[...])
    is_end = jnp.logical_or(r == 0, r == n_dp - 1)
    which = jnp.where(is_end, 0, 1)
    across = jnp.where(r < 2, 2, 1)

    def raw_copies(j):
        return [
            pltpu.make_async_remote_copy(
                src_ref=source, dst_ref=held.at[j],
                send_sem=raw_send.at[i], recv_sem=raw_recv.at[i, j],
                device_id={"dp": across}, device_id_type=MESH,
            )
            for i, (source, held) in enumerate(((ids_ref, raw_ids), (tokens_ref, raw)))
        ]

    def far_block(j, e):
        return pl.ds(pl.multiple_of((1 + j) * slots + e * cap, cap), cap)

    def far_exchange(j, to, at, peer_id=None):
        return pltpu.make_async_remote_copy(
            src_ref=far_sent.at[j, block(to)],
            dst_ref=got.at[0, far_block(j, at)],
            send_sem=far_send.at[j, to],
            recv_sem=far_recv.at[j, at],
            device_id={"expert": to if peer_id is None else peer_id},
            device_id_type=MESH,
        )

    def slice_copy(j):
        own = pl.ds(pl.multiple_of(jnp.where(r < 2, 2 * part, 0), part), 2 * part)
        return pltpu.make_async_remote_copy(
            src_ref=da_t.at[own, pl.ds(0, slots)],
            dst_ref=da_t.at[own, pl.ds(pl.multiple_of((1 + j) * slots, slots), slots)],
            send_sem=slice_send,
            recv_sem=slice_recv.at[j],
            device_id={"dp": across},
            device_id_type=MESH,
        )

    def slice_wait(j):
        own = pl.ds(pl.multiple_of(jnp.where(r < 2, 0, 2 * part), part), 2 * part)
        far = pl.ds(pl.multiple_of((1 + j) * slots, slots), slots)
        return pltpu.make_async_remote_copy(
            src_ref=da_t.at[own, pl.ds(0, slots)],
            dst_ref=da_t.at[own, far],
            send_sem=slice_send,
            recv_sem=slice_recv.at[j],
            device_id={"dp": across},
            device_id_type=MESH,
        )

    partner = r + 1 - 2 * lax.rem(r, 2)

    def pair_copy(c):
        return pltpu.make_async_remote_copy(
            src_ref=pair_out.at[c], dst_ref=pair_in.at[c],
            send_sem=pair_send.at[c], recv_sem=pair_recv.at[c],
            device_id={"dp": partner}, device_id_type=MESH,
        )

    sent[0] = jnp.dot(place, tokens_ref[...], preferred_element_type=F32).astype(BF16)
    pl.semaphore_wait(barrier, n_exp - 1 + n_dp - 1)

    def exchange(t, k):
        to = peer(k)
        return pltpu.make_async_remote_copy(
            src_ref=sent.at[t, block(to)],
            dst_ref=got.at[t, block(me)],
            send_sem=send_sem.at[t, to],
            recv_sem=recv_sem.at[t, me],
            device_id={"expert": to},
            device_id_type=MESH,
        )

    def arrival(t, k):
        of = peer(k)
        return pltpu.make_async_remote_copy(
            src_ref=sent.at[t, block(of)],
            dst_ref=got.at[t, block(of)],
            send_sem=send_sem.at[t, of],
            recv_sem=recv_sem.at[t, of],
            device_id={"expert": of},
            device_id_type=MESH,
        )

    @pl.loop(1, n_exp)
    def _(k):
        exchange(0, k).start()

    if deep:
        for copy in raw_copies(which):
            copy.start()

    got[0, block(me)] = sent[0, block(me)]
    weights = jnp.transpose(
        jnp.broadcast_to(weights_ref[...].astype(F32), (LANES, rows))
    )[:, 0:1]
    scaled = (weights * grads_ref[...].astype(F32)).astype(BF16)
    sent[1] = jnp.dot(place, scaled, preferred_element_type=F32).astype(BF16)

    @pl.loop(1, n_exp)
    def _(k):
        exchange(1, k).start()

    got[1, block(me)] = sent[1, block(me)]

    for load in loads:
        load.wait()

    end = jnp.logical_or(r == 0, r == n_dp - 1)
    after_end = jnp.logical_or(r == 1, r == n_dp - 2)
    inner = jnp.where(r == 0, up, low)
    lower = r < n_dp // 2

    def hand_x(e):
        return pltpu.make_async_remote_copy(
            src_ref=got.at[first, block(e)],
            dst_ref=got.at[first, pl.ds(pl.multiple_of(slots + e * cap, cap), cap)],
            send_sem=x_send.at[e],
            recv_sem=x_recv.at[e],
            device_id={"dp": inner},
            device_id_type=MESH,
        )

    def hand_g(c):
        span = pl.ds(pl.multiple_of(c * piece, piece), piece)
        return pltpu.make_async_remote_copy(
            src_ref=got.at[1, pl.ds(0, slots), span],
            dst_ref=got.at[1, pl.ds(slots, slots), span],
            send_sem=g_send.at[c],
            recv_sem=g_recv.at[c],
            device_id={"dp": inner},
            device_id_type=MESH,
        )

    def hand_cut(t, d):
        left = da_t if t == 0 else hid_t
        own = pl.ds(pl.multiple_of(d * part, part), part)
        return pltpu.make_async_remote_copy(
            src_ref=left.at[own, pl.ds(0, slots)],
            dst_ref=left.at[own, pl.ds(slots, slots)],
            send_sem=cut_send.at[t, d],
            recv_sem=cut_recv.at[t, d],
            device_id={"dp": inner},
            device_id_type=MESH,
        )

    first = 1 if deep else 0

    @pl.when(end)
    def _():
        hand_x(me).start()

    @pl.loop(1, n_exp)
    def _(k):
        arrival(0, k).wait_recv()

        if not deep:

            @pl.when(end)
            def _():
                hand_x(peer(k)).start()

    nt = (((1,), (1,)), ((), ()))

    @pl.loop(0, units // tile)
    def _(j):
        span = pl.ds(pl.multiple_of(j * tile, tile), tile)
        value = lax.dot_general(
            gate[span, :], got[0, 0:slots, :], nt, preferred_element_type=F32
        )
        preact[span, :] = value
        hid_t[span, 0:slots] = (value * jax.nn.sigmoid(value)).astype(BF16)

    def hand_cuts(t):
        @pl.when(end)
        def _():
            @pl.loop(0, n_dp - 1)
            def _(j):
                hand_cut(t, jnp.where(r == 0, n_dp - 1 - j, j)).start()

    if deep:
        hand_cuts(1)

    @pl.loop(1, n_exp)
    def _(k):
        arrival(1, k).wait_recv()

        if deep:

            @pl.when(end)
            def _():
                hand_x(peer(k)).start()

    def second(j, total):
        span = pl.ds(pl.multiple_of(j * tile, tile), tile)
        slope = lax.dot_general(
            down[span, :], got[1, 0:slots, :], nt, preferred_element_type=F32
        )
        value = preact[span, :]
        sigma = jax.nn.sigmoid(value)
        da_t[span, 0:slots] = (slope * (sigma * (1.0 + value * (1.0 - sigma)))).astype(BF16)
        return total + jnp.sum(hid_t[span, 0:slots].astype(F32) * slope, axis=0, keepdims=True)

    route = lax.fori_loop(0, units // tile, second, jnp.zeros((1, slots), F32))

    if deep:
        slice_copy(which).start()

        @pl.when(after_end)
        def _():
            for j in (1, 0):
                for copy in raw_copies(j):
                    copy.wait_recv()
                far_sent[j] = jnp.dot(
                    placement(raw_ids[j]), raw[j], preferred_element_type=F32
                ).astype(BF16)

                @pl.loop(1, n_exp)
                def _(k):
                    far_exchange(j, peer(k), me).start()

                got[0, far_block(j, me)] = far_sent[j, block(me)]
    else:
        hand_cuts(0)
        hand_cuts(1)

        @pl.when(end)
        def _():
            @pl.loop(0, pieces)
            def _(c):
                hand_g(c).start()

    def term(t, d, span, wide):
        left = da_t if t == 0 else hid_t
        start = d * part if isinstance(d, int) else pl.multiple_of(d * part, part)
        depth = (3 if deep and t == 0 else 2) * slots if wide else slots
        return jnp.dot(
            left[pl.ds(start, part), 0:depth],
            got[t, 0:depth, span],
            preferred_element_type=F32,
        )

    def columns(c):
        return pl.ds(pl.multiple_of(c * piece, piece), piece)

    def hop(buf, s_sem, r_sem, t, d, c, to):
        return pltpu.make_async_remote_copy(
            src_ref=buf.at[t, d, c],
            dst_ref=buf.at[t, d, c],
            send_sem=s_sem.at[t, d, c],
            recv_sem=r_sem.at[t, d, c],
            device_id={"dp": to},
            device_id_type=MESH,
        )

    def rightward(t, d, c, to=None):
        return hop(right_buf, r_send, r_recv, t, d - 1, c, up)

    def leftward(t, d, c, to=None):
        return hop(left_buf, l_send, l_recv, t, d, c, low)

    def pass_on(t, d, c, copy, buf, index, first):
        @pl.when(first)
        def _():
            buf[t, index, c] = term(t, d, columns(c), True).astype(BF16)

        @pl.when(jnp.logical_not(first))
        def _():
            own = term(t, d, columns(c), False)
            copy.wait_recv()
            buf[t, index, c] = (own + buf[t, index, c].astype(F32)).astype(BF16)

        copy.start()

    def go_right(t):
        for d in range(n_dp - 1, 1, -1):

            @pl.when(r == 1)
            def _():
                hand_cut(t, d).wait_recv()

            @pl.when(jnp.logical_and(r > 0, r < d))
            def _():
                @pl.loop(0, pieces)
                def _(c):
                    if not deep and t == 1 and d == n_dp - 1:

                        @pl.when(r == 1)
                        def _():
                            hand_g(c).wait_recv()

                    pass_on(t, d, c, rightward(t, d, c), right_buf, d - 1, r == 1)

    def go_left(t):
        for d in range(n_dp - 2):

            @pl.when(r == n_dp - 2)
            def _():
                hand_cut(t, d).wait_recv()

            @pl.when(jnp.logical_and(r < n_dp - 1, r > d))
            def _():
                @pl.loop(0, pieces)
                def _(c):
                    if not deep and t == 1 and d == 0:

                        @pl.when(r == n_dp - 2)
                        def _():
                            hand_g(c).wait_recv()

                    pass_on(t, d, c, leftward(t, d, c), left_buf, d, r == n_dp - 2)

    def returning(k):
        to = peer(k)
        return pltpu.make_async_remote_copy(
            src_ref=back.at[block(to)],
            dst_ref=returned.at[block(me)],
            send_sem=back_send.at[to],
            recv_sem=back_recv.at[me],
            device_id={"expert": to},
            device_id_type=MESH,
        )

    def homecoming(k):
        of = peer(k)
        return pltpu.make_async_remote_copy(
            src_ref=back.at[block(of)],
            dst_ref=returned.at[block(of)],
            send_sem=back_send.at[of],
            recv_sem=back_recv.at[of],
            device_id={"expert": of},
            device_id_type=MESH,
        )

    def send_back():
        tn = (((0,), (0,)), ((), ()))

        @pl.loop(0, pieces)
        def _(c):
            span = columns(c)
            back[:, span] = lax.dot_general(
                da_t[:, 0:slots], gate[:, span], tn, preferred_element_type=F32
            ).astype(BF16)

        tall = jnp.transpose(jnp.broadcast_to(route, (LANES, slots)))
        high = tall.astype(BF16)
        rest = (tall - high.astype(F32)).astype(BF16)
        lane = lax.broadcasted_iota(jnp.int32, (slots, LANES), 1)
        back[:, pl.ds(width, LANES)] = jnp.where(
            lane < 1, high.astype(F32), rest.astype(F32)
        ).astype(BF16)

        @pl.loop(1, n_exp)
        def _(k):
            returning(k).start()

        returned[block(me), :] = back[block(me), :]

    send_back()

    @pl.when(after_end)
    def _():
        @pl.loop(0, n_exp)
        def _(e):
            hand_x(e).wait_recv()

    for t in range(first, 2):

        @pl.when(lower)
        def _():
            go_right(t)

        go_left(t)

        @pl.when(jnp.logical_not(lower))
        def _():
            go_right(t)

    if deep:

        @pl.when(after_end)
        def _():
            for j in (1, 0):
                slice_wait(j).wait_recv()

                @pl.loop(1, n_exp)
                def _(k):
                    far_exchange(j, me, peer(k), peer(k)).wait_recv()

        @pl.loop(0, pieces)
        def _(c):
            for wide, role in ((True, after_end), (False, end)):

                @pl.when(role)
                def _():
                    pair_out[c] = term(0, partner, columns(c), wide).astype(BF16)

            pair_copy(c).start()

    @pl.loop(1, n_exp)
    def _(k):
        homecoming(k).wait_recv()

    tn = (((0,), (0,)), ((), ()))

    @pl.loop(0, pieces)
    def _(c):
        span = columns(c)
        token_out[:, span] = lax.dot_general(
            place, returned[:, span], tn, preferred_element_type=F32
        ).astype(BF16)

    pair = lax.dot_general(
        place, returned[:, pl.ds(width, LANES)], tn, preferred_element_type=F32
    )
    total = jnp.broadcast_to((pair[:, 0:1] + pair[:, 1:2]) / weights, (rows, LANES))
    route_out[...] = jnp.transpose(total)[0:1, :].astype(BF16)

    if deep:

        @pl.loop(0, pieces)
        def _(c):
            span = columns(c)
            for wide, role in ((True, after_end), (False, end)):

                @pl.when(role)
                def _():
                    own = term(0, r, span, wide)
                    pair_copy(c).wait_recv()
                    gate_out[:, span] = (own + pair_in[c].astype(F32)).astype(BF16)

    for t in range(first, 2):
        out = gate_out if t == 0 else down_out

        @pl.when(after_end)
        def _():
            hand_cut(t, r).wait_recv()

        @pl.loop(0, pieces)
        def _(c):
            span = columns(c)

            def from_right():
                hop(left_buf, l_send, l_recv, t, r, c, low).wait_recv()
                return left_buf[t, r, c].astype(F32)

            def from_left():
                hop(right_buf, r_send, r_recv, t, r - 1, c, up).wait_recv()
                return right_buf[t, r - 1, c].astype(F32)

            @pl.when(r == 0)
            def _():
                out[:, span] = (term(t, r, span, False) + from_right()).astype(BF16)

            @pl.when(r == n_dp - 1)
            def _():
                out[:, span] = (term(t, r, span, False) + from_left()).astype(BF16)

            @pl.when(r == 1)
            def _():
                out[:, span] = (term(t, r, span, True) + from_right()).astype(BF16)

            @pl.when(r == n_dp - 2)
            def _():
                out[:, span] = (term(t, r, span, True) + from_left()).astype(BF16)

            @pl.when(jnp.logical_and(r > 1, r < n_dp - 2))
            def _():
                out[:, span] = (term(t, r, span, False) + from_right() + from_left()).astype(BF16)

    @pl.loop(1, n_exp)
    def _(k):
        exchange(0, k).wait_send()
        exchange(1, k).wait_send()
        returning(k).wait_send()

    @pl.when(end)
    def _():
        @pl.loop(0, n_exp)
        def _(e):
            hand_x(e).wait_send()

        if not deep:

            @pl.loop(0, pieces)
            def _(c):
                hand_g(c).wait_send()

        for t in range(first, 2):

            @pl.loop(0, n_dp - 1)
            def _(j):
                hand_cut(t, jnp.where(r == 0, n_dp - 1 - j, j)).wait_send()

    if deep:
        for copy in raw_copies(which):
            copy.wait_send()
        slice_copy(which).wait_send()

        @pl.loop(0, pieces)
        def _(c):
            pair_copy(c).wait_send()

        @pl.when(after_end)
        def _():
            for j in (1, 0):

                @pl.loop(1, n_exp)
                def _(k):
                    far_exchange(j, peer(k), me).wait_send()

    for t in range(first, 2):
        for d in range(n_dp):

            @pl.loop(0, pieces)
            def _(c):
                if d > 1:

                    @pl.when(jnp.logical_and(r > 0, r < d))
                    def _():
                        rightward(t, d, c).wait_send()

                if d < n_dp - 2:

                    @pl.when(jnp.logical_and(r < n_dp - 1, r > d))
                    def _():
                        leftward(t, d, c).wait_send()


def settle(*refs):
    half = len(refs) // 2
    for source, out in zip(refs[:half], refs[half:]):
        out[...] = source[...]


def per_device(tokens, expert_ids, route_weights, out_grad, gate_weight, down_weight):
    rows, width = tokens.shape
    n_exp, n_dp = lax.axis_size("expert"), lax.axis_size("dp")
    top = expert_ids.shape[1]
    assert top == 1 and n_dp >= 4
    cap = -(-max(2, 2 * rows * top // n_exp) // 16) * 16
    slots = n_exp * cap
    units = gate_weight.shape[1]
    part = units // n_dp
    pieces = max(1, width // 512)
    piece = width // pieces
    deep = n_dp == 4
    copies = 3 if deep else 2
    vmem = pl.BlockSpec(memory_space=pltpu.VMEM)
    hbm = pl.BlockSpec(memory_space=pl.ANY)
    results = pl.pallas_call(
        functools.partial(kernel, n_dp, n_exp, cap, pieces),
        out_shape=(
            jax.ShapeDtypeStruct((rows, width), BF16),
            jax.ShapeDtypeStruct((1, rows), BF16),
            jax.ShapeDtypeStruct((part, width), BF16),
            jax.ShapeDtypeStruct((part, width), BF16),
        ),
        in_specs=[vmem, vmem, vmem, vmem, hbm, hbm],
        out_specs=(vmem, vmem, vmem, vmem),
        scratch_shapes=[
            pltpu.VMEM((2, slots, width), BF16),
            pltpu.VMEM((2, copies * slots, width), BF16),
            pltpu.VMEM((units, width), BF16),
            pltpu.VMEM((units, width), BF16),
            pltpu.VMEM((units, slots), F32),
            pltpu.VMEM((units, copies * slots), BF16),
            pltpu.VMEM((units, copies * slots), BF16),
            pltpu.VMEM((slots, width + LANES), BF16),
            pltpu.VMEM((slots, width + LANES), BF16),
            pltpu.VMEM((2, n_dp - 1, pieces, part, piece), BF16),
            pltpu.VMEM((2, n_dp - 1, pieces, part, piece), BF16),
            pltpu.SemaphoreType.DMA((2,)),
            pltpu.SemaphoreType.DMA((2, n_exp)),
            pltpu.SemaphoreType.DMA((2, n_exp)),
            pltpu.SemaphoreType.DMA((n_exp,)),
            pltpu.SemaphoreType.DMA((n_exp,)),
            pltpu.SemaphoreType.DMA((2, n_dp - 1, pieces)),
            pltpu.SemaphoreType.DMA((2, n_dp - 1, pieces)),
            pltpu.SemaphoreType.DMA((2, n_dp - 1, pieces)),
            pltpu.SemaphoreType.DMA((2, n_dp - 1, pieces)),
            pltpu.SemaphoreType.DMA((n_exp,)),
            pltpu.SemaphoreType.DMA((n_exp,)),
            pltpu.SemaphoreType.DMA((pieces,)),
            pltpu.SemaphoreType.DMA((pieces,)),
            pltpu.SemaphoreType.DMA((2, n_dp)),
            pltpu.SemaphoreType.DMA((2, n_dp)),
            pltpu.VMEM((2, rows, width) if deep else (2, 16, LANES), BF16),
            pltpu.VMEM((2, 1, rows), jnp.int32),
            pltpu.VMEM((2, slots, width) if deep else (2, 16, LANES), BF16),
            pltpu.VMEM((pieces, part, piece) if deep else (1, 16, LANES), BF16),
            pltpu.VMEM((pieces, part, piece) if deep else (1, 16, LANES), BF16),
            pltpu.SemaphoreType.DMA((2,)),
            pltpu.SemaphoreType.DMA((2, 2)),
            pltpu.SemaphoreType.DMA((2, n_exp)),
            pltpu.SemaphoreType.DMA((2, n_exp)),
            pltpu.SemaphoreType.DMA,
            pltpu.SemaphoreType.DMA((2,)),
            pltpu.SemaphoreType.DMA((pieces,)),
            pltpu.SemaphoreType.DMA((pieces,)),
        ],
        compiler_params=pltpu.CompilerParams(
            collective_id=0, has_side_effects=True, vmem_limit_bytes=46_000_000 if deep else 67_000_000
        ),
    )(
        expert_ids.reshape(1, rows), tokens, route_weights.reshape(1, rows), out_grad,
        gate_weight[0], down_weight[0],
    )
    token_grad, route_grad, gate_grad, down_grad = pl.pallas_call(
        settle,
        out_shape=tuple(jax.ShapeDtypeStruct(a.shape, a.dtype) for a in results),
        in_specs=[vmem] * 4,
        out_specs=(vmem,) * 4,
    )(*results)
    return token_grad, route_grad.reshape(rows, 1), gate_grad[None], down_grad[None]


def solution(mesh):
    placed = (
        P(("dp", "expert"), None),
        P(("dp", "expert"), None),
        P(("dp", "expert"), None),
        P(("dp", "expert"), None),
        P("expert", None, None),
        P("expert", None, None),
    )
    return jax.shard_map(
        per_device,
        mesh=mesh,
        in_specs=placed,
        out_specs=(
            P(("dp", "expert"), None),
            P(("dp", "expert"), None),
            P("expert", "dp", None),
            P("expert", "dp", None),
        ),
        check_vma=False,
    )
```
